256 devices in a mesh: pipe: 4 (over y_hi, core), expert: 64 (over y_lo, z, x).
Axes of the slice: x: 4, y: 4 (y_hi: 2, y_lo: 2; y = y_hi * 2 + y_lo), z: 8, core: 2. Of those that a mesh axis runs over, the one named last changes fastest.
Arguments:
- tokens: bfloat16 [8192, 7168], P('expert', 'pipe'), may hold values from -6 to 6
- grad_out: bfloat16 [8192, 7168], P('expert', 'pipe'), may hold values from -6 to 6
- routed_expert_index: int32 [8192, 8], P('expert'), may hold values from 0 to 255, as said below
- route_gates: bfloat16 [8192, 8], P('expert'), may hold values from 0.099609375 to 0.5
- gate_up: bfloat16 [2, 7168, 8192], P(None, 'pipe', 'expert'), may hold values from -0.0625 to 0.0625
- gate_up_m: bfloat16 [2, 7168, 8192], P(None, 'pipe', 'expert'), may hold values from -24 to 24
- gate_up_v: bfloat16 [2, 7168, 8192], P(None, 'pipe', 'expert'), may hold values from 4 to 400
- down: bfloat16 [8192, 7168], P('expert', 'pipe'), may hold values from -0.1875 to 0.1875
- down_m: bfloat16 [8192, 7168], P('expert', 'pipe'), may hold values from -12 to 12
- down_v: bfloat16 [8192, 7168], P('expert', 'pipe'), may hold values from 1 to 100
Outputs:
- mixed: bfloat16 [8192, 7168], P('expert', 'pipe')
- grad_tokens: bfloat16 [8192, 7168], P('expert', 'pipe')
- gate_up_new: bfloat16 [2, 7168, 8192], P(None, 'pipe', 'expert')
- gate_up_m_new: bfloat16 [2, 7168, 8192], P(None, 'pipe', 'expert')
- gate_up_v_new: bfloat16 [2, 7168, 8192], P(None, 'pipe', 'expert')
- down_new: bfloat16 [8192, 7168], P('expert', 'pipe')
- down_m_new: bfloat16 [8192, 7168], P('expert', 'pipe')
- down_v_new: bfloat16 [8192, 7168], P('expert', 'pipe')
The draws below stay inside these ranges and needn't reach their ends.
Inputs may be any that keep to these rules, and one draw needn't show every extreme that they name: `routed_expert_index`: each token names 8 different experts. In each aligned block of 128 tokens, every expert below 8 is named by 1 to 16 of the tokens, and one of them by exactly 16.
All inputs are finite; a program needn't handle non-finite values.
Results may differ from the reference program's by a relative error of at most 0.0058.
Values may be sent and summed in bfloat16 or wider, within the bound.
No kernel may reach another device: no remote copies, remote signals or barrier semaphores. Data moves between devices by JAX's collectives and lax.ppermute only.
A program may use at most 128 MiB of HBM per device.

```python
import math
import jax
import jax.numpy as jnp
from jax import lax

D = 7168
TOP = 8
FF = 1024
GROUP = 8
TOK_DEV = 128
HID_DEV = 128
EXPERT_COUNT = 8
ALL_EXPERTS = 256
TOKENS = 8192
CAP = 16


def draw_routed_expert_index(key, part):
    blocks = TOKENS // TOK_DEV
    key_limit, key_count, key_peak, key_rank, key_other, key_order = jax.random.split(key, 6)
    shifts = jax.random.randint(key_limit, (EXPERT_COUNT,), 0, 2)
    limits = jnp.maximum(CAP // jnp.power(2, shifts), 1)
    counts = jax.random.randint(key_count, (blocks, EXPERT_COUNT), 0, 1 << 20) % limits[None, :] + 1
    peak = jax.random.randint(key_peak, (blocks,), 0, EXPERT_COUNT)
    expert_iota = jnp.arange(EXPERT_COUNT, dtype=jnp.int32)
    counts = jnp.where(expert_iota[None, :] == peak[:, None], CAP, counts)
    token_iota = jnp.arange(TOK_DEV, dtype=jnp.int32)
    rank_keys = jax.random.randint(key_rank, (blocks, EXPERT_COUNT, TOK_DEV), 0, 1 << 20) * TOK_DEV + token_iota
    ordering = jnp.argsort(rank_keys, axis=-1)
    ranking = jnp.argsort(ordering, axis=-1)
    member = ranking < counts[:, :, None]
    near_scores = jnp.where(jnp.transpose(member, (0, 2, 1)), (1 << 28) + expert_iota, -1 - expert_iota)
    far_count = ALL_EXPERTS - EXPERT_COUNT
    far_scores = jax.random.randint(key_other, (blocks, TOK_DEV, far_count), 0, 1 << 16) * ALL_EXPERTS + jnp.arange(EXPERT_COUNT, ALL_EXPERTS, dtype=jnp.int32)
    scores = jnp.concatenate((near_scores.astype(jnp.int32), far_scores.astype(jnp.int32)), axis=-1)
    unused_values, chosen = lax.top_k(scores, TOP)
    shuffle_keys = jax.random.randint(key_order, (blocks, TOK_DEV, TOP), 0, 1 << 20) * TOP + jnp.arange(TOP, dtype=jnp.int32)
    shuffle = jnp.argsort(shuffle_keys, axis=-1)
    chosen = jnp.take_along_axis(chosen, shuffle, axis=-1)
    return chosen.reshape(TOKENS, TOP).astype(jnp.int32)


def shard_levels(own_key, dims, cuts, smallest, top_value):
    gain, own = 1.0, jax.random.fold_in(own_key, 6)
    for dim, shards_of in cuts:
        heights = jnp.exp(jax.random.uniform(jax.random.fold_in(own, dim), (shards_of,), jnp.float32, smallest / len(cuts), top_value / len(cuts)))
        gain = gain * jnp.repeat(heights, dims[dim] // shards_of).reshape([-1 if axis == dim else 1 for axis in range(len(dims))])
    return gain


def scatter_about(key, dims, width, bound, cuts=(), kind=jnp.bfloat16):
    array = width * jax.random.normal(key, dims, jnp.float32)
    if cuts:
        array = array * shard_levels(key, dims, cuts, -0.22, 0.18)
    return jnp.clip(array, -bound, bound).astype(kind)


def setup_inputs(seed: int = 0) -> dict:
    key_of = jax.random.split(jax.random.key(seed), 11)
    tokens = scatter_about(key_of[0], (TOKENS, D), 1.0, 6.0, ((0, 64), (1, 4)))
    grad_out = scatter_about(key_of[1], (TOKENS, D), 1.0, 6.0, ((0, 64), (1, 4)))
    routed_expert_index = draw_routed_expert_index(jax.random.fold_in(key_of[10], 71), 0)
    route_gates = jnp.clip(0.099609375 + 0.40039062 * jax.random.uniform(key_of[3], (TOKENS, TOP), jnp.float32) ** shard_levels(key_of[3], (TOKENS, TOP), ((0, 64),), -0.2, 0.2), 0.099609375, 0.5).astype(jnp.bfloat16)
    gate_up = scatter_about(key_of[4], (2, D, EXPERT_COUNT * FF), D ** -0.5, 0.0625, ((1, 4), (2, 64)))
    gate_up_m = scatter_about(key_of[5], (2, D, EXPERT_COUNT * FF), 4.0, 24.0, ((1, 4), (2, 64)))
    gate_up_v = jnp.clip(jnp.exp(math.log(400.0) - 4.6051702 * jax.random.uniform(key_of[6], (2, D, EXPERT_COUNT * FF), jnp.float32) ** shard_levels(key_of[6], (2, D, EXPERT_COUNT * FF), ((1, 4), (2, 64)), -0.2, 0.2)), 4.0, 400.0).astype(jnp.bfloat16)
    down = scatter_about(key_of[7], (EXPERT_COUNT * FF, D), FF ** -0.5, 0.1875, ((0, 64), (1, 4)))
    down_m = scatter_about(key_of[8], (EXPERT_COUNT * FF, D), 2.0, 12.0, ((0, 64), (1, 4)))
    down_v = jnp.clip(jnp.exp(math.log(100.0) - 4.6051702 * jax.random.uniform(key_of[9], (EXPERT_COUNT * FF, D), jnp.float32) ** shard_levels(key_of[9], (EXPERT_COUNT * FF, D), ((0, 64), (1, 4)), -0.2, 0.2)), 1.0, 100.0).astype(jnp.bfloat16)
    return {"tokens": tokens, "grad_out": grad_out, "routed_expert_index": routed_expert_index, "route_gates": route_gates, "gate_up": gate_up, "gate_up_m": gate_up_m, "gate_up_v": gate_up_v, "down": down, "down_m": down_m, "down_v": down_v}


beta_first = 0.9
beta_second = 0.95
learning_rate = 0.00022
decay_rate = 0.1
epsilon = 1e-08

def adamw(weight, moment_one, moment_two, gradient):
    weight_real = weight.astype(jnp.float32)
    first_new = beta_first * moment_one.astype(jnp.float32) + (1.0 - beta_first) * gradient
    second_new = beta_second * moment_two.astype(jnp.float32) + (1.0 - beta_second) * gradient * gradient
    weight_new = weight_real - learning_rate * (first_new / (jnp.sqrt(second_new) + epsilon) + decay_rate * weight_real)
    return (weight_new.astype(jnp.bfloat16), first_new.astype(jnp.bfloat16), second_new.astype(jnp.bfloat16))

def reference(tokens, grad_out, routed_expert_index, route_gates, gate_up, gate_up_m, gate_up_v, down, down_m, down_v):
    blocks = TOKENS // TOK_DEV
    rows_all = blocks * CAP
    grouped_rows = routed_expert_index.reshape(blocks, TOK_DEV, TOP)
    onehot = (grouped_rows[..., None] == jnp.arange(EXPERT_COUNT, dtype=jnp.int32)).astype(jnp.int32)
    per_token = lax.optimization_barrier(jnp.sum(onehot, axis=2))
    before = jnp.cumsum(per_token, axis=1) - per_token
    slot_index = lax.optimization_barrier(jnp.sum(onehot * before[:, :, None, :], axis=3))
    active_experts = grouped_rows < EXPERT_COUNT
    block_offset = (jnp.arange(blocks, dtype=jnp.int32) * CAP)[:, None, None]
    slot_positions = jnp.where(active_experts, block_offset + slot_index, 0).astype(jnp.int32)
    target_rows = jnp.where(active_experts, grouped_rows, EXPERT_COUNT).astype(jnp.int32)
    token_index = jnp.broadcast_to(jnp.arange(TOKENS, dtype=jnp.int32).reshape(blocks, TOK_DEV, 1), grouped_rows.shape)
    token_table = jnp.full((EXPERT_COUNT + 1, rows_all), -1, jnp.int32)
    token_table = token_table.at[target_rows.ravel(), slot_positions.ravel()].set(token_index.ravel())[:EXPERT_COUNT]
    gate_table = jnp.zeros((EXPERT_COUNT + 1, rows_all), jnp.float32)
    gate_table = gate_table.at[target_rows.ravel(), slot_positions.ravel()].set(route_gates.reshape(-1).astype(jnp.float32))[:EXPERT_COUNT]
    paired_weights = gate_up.reshape(2, D, EXPERT_COUNT, FF).transpose(2, 0, 1, 3)
    down_weights = down.reshape(EXPERT_COUNT, FF, D)

    def expert_step(accums, inputs):
        mixed_acc, grad_acc = accums
        token_row, gate_row, pair_weight, down_weight = inputs
        filled = token_row >= 0
        safe_index = jnp.where(filled, token_row, 0)
        row_data = jnp.where(filled[:, None], tokens[safe_index], jnp.zeros((), jnp.bfloat16))
        grad_rows = jnp.where(filled[:, None], grad_out[safe_index], jnp.zeros((), jnp.bfloat16))
        gate_pre = jnp.dot(row_data, pair_weight[0], preferred_element_type=jnp.float32)
        up_pre = jnp.dot(row_data, pair_weight[1], preferred_element_type=jnp.float32)
        scaled = (gate_row[:, None] * jax.nn.silu(gate_pre) * up_pre).astype(jnp.bfloat16)
        back_prop = jnp.dot(grad_rows, down_weight.T, preferred_element_type=jnp.float32)
        d_hidden = gate_row[:, None] * back_prop
        sigmoid_gate = jax.nn.sigmoid(gate_pre)
        d_gate = (d_hidden * up_pre * sigmoid_gate * (1.0 + gate_pre * (1.0 - sigmoid_gate))).astype(jnp.bfloat16)
        d_up = (d_hidden * gate_pre * sigmoid_gate).astype(jnp.bfloat16)
        out_rows = jnp.zeros((rows_all, D), jnp.float32)
        back_rows = jnp.zeros((rows_all, D), jnp.float32)
        for part_index in range(GROUP):
            col_start = part_index * HID_DEV
            col_end = col_start + HID_DEV
            piece = jnp.dot(scaled[:, col_start:col_end], down_weight[col_start:col_end], preferred_element_type=jnp.float32)
            out_rows = out_rows + lax.optimization_barrier(piece.astype(jnp.bfloat16)).astype(jnp.float32)
            back_piece = jnp.dot(d_gate[:, col_start:col_end], pair_weight[0][:, col_start:col_end].T, preferred_element_type=jnp.float32)
            back_piece = back_piece + jnp.dot(d_up[:, col_start:col_end], pair_weight[1][:, col_start:col_end].T, preferred_element_type=jnp.float32)
            back_rows = back_rows + lax.optimization_barrier(back_piece.astype(jnp.bfloat16)).astype(jnp.float32)
        mask_real = filled.astype(jnp.float32)[:, None]
        mixed_acc = mixed_acc.at[safe_index].add(out_rows * mask_real)
        grad_acc = grad_acc.at[safe_index].add(back_rows * mask_real)
        grad_gate = jnp.dot(row_data.T, d_gate, preferred_element_type=jnp.float32)
        grad_up = jnp.dot(row_data.T, d_up, preferred_element_type=jnp.float32)
        grad_down = jnp.dot(scaled.T, grad_rows, preferred_element_type=jnp.float32)
        return ((mixed_acc, grad_acc), (jnp.stack((grad_gate, grad_up)), grad_down))
    start_accums = (jnp.zeros((TOKENS, D), jnp.float32), jnp.zeros((TOKENS, D), jnp.float32))
    (mixed_acc, grad_acc), (grad_pairs, grad_downs) = lax.scan(expert_step, start_accums, (token_table, gate_table, paired_weights, down_weights))
    grad_gate_up = grad_pairs.transpose(1, 2, 0, 3).reshape(2, D, EXPERT_COUNT * FF)
    grad_down_all = grad_downs.reshape(EXPERT_COUNT * FF, D)
    gate_up_new, gate_up_m_new, gate_up_v_new = adamw(gate_up, gate_up_m, gate_up_v, grad_gate_up)
    down_new, down_m_new, down_v_new = adamw(down, down_m, down_v, grad_down_all)
    return (mixed_acc.astype(jnp.bfloat16), grad_acc.astype(jnp.bfloat16), gate_up_new, gate_up_m_new, gate_up_v_new, down_new, down_m_new, down_v_new)
```

```python
import jax
import jax.numpy as jnp
from jax import lax
from jax.sharding import Mesh
from jax.sharding import PartitionSpec as P

GROUP = 8


beta_first = 0.9
beta_second = 0.95
learning_rate = 0.00022
decay_rate = 0.1
epsilon = 1e-08


def adamw(weight, moment_one, moment_two, gradient):
    weight_real = weight.astype(jnp.float32)
    first_new = beta_first * moment_one.astype(jnp.float32) + (1.0 - beta_first) * gradient
    second_new = (
        beta_second * moment_two.astype(jnp.float32) + (1.0 - beta_second) * gradient * gradient
    )
    weight_new = weight_real - learning_rate * (
        first_new / (jnp.sqrt(second_new) + epsilon) + decay_rate * weight_real
    )
    return (
        weight_new.astype(jnp.bfloat16),
        first_new.astype(jnp.bfloat16),
        second_new.astype(jnp.bfloat16),
    )


def f32_dot(left, right, dims):
    return lax.dot_general(left, right, (dims, ((), ())), preferred_element_type=jnp.float32)


def swap(value, axis):
    return lax.ppermute(value, axis, [(0, 1), (1, 0)])


def shift(value, step):
    size = lax.axis_size("x")
    return lax.ppermute(value, "x", [(i, (i + step) % size) for i in range(size)])


def to_bf16(value):
    return value.astype(jnp.bfloat16)


def per_device(
    tokens,
    grad_out,
    routed_expert_index,
    route_gates,
    gate_up,
    gate_up_m,
    gate_up_v,
    down,
    down_m,
    down_v,
):
    expert_list = lax.axis_size("y_lo") * lax.axis_size("z_hi")
    tok_dev, width_dev = tokens.shape
    hidden = gate_up.shape[2]
    capacity = 16
    rows = expert_list * capacity

    experts = jnp.arange(expert_list, dtype=jnp.int32)[:, None, None]
    index_t = routed_expert_index.T
    gates_t = route_gates.T.astype(jnp.float32)
    named = (index_t[None] == experts).astype(jnp.float32)
    member = jnp.sum(named, axis=1)
    gate_of = jnp.sum(named * gates_t[None], axis=1)
    earlier = (
        lax.broadcasted_iota(jnp.int32, (tok_dev, tok_dev), 0)
        < lax.broadcasted_iota(jnp.int32, (tok_dev, tok_dev), 1)
    ).astype(jnp.bfloat16)
    slot = f32_dot(to_bf16(member), earlier, ((1,), (0,))).astype(jnp.int32)
    slots = lax.broadcasted_iota(jnp.int32, (expert_list, capacity, tok_dev), 1)
    here = (slots == slot[:, None, :]) & (member[:, None, :] > 0.5)
    selector = here.astype(jnp.bfloat16).reshape(rows, tok_dev)
    gate_selector = to_bf16(jnp.where(here, gate_of[:, None, :], 0.0)).reshape(rows, tok_dev)

    tok_rows = to_bf16(f32_dot(selector, tokens, ((1,), (0,))))
    grad_rows = to_bf16(f32_dot(gate_selector, grad_out, ((1,), (0,))))
    send = jnp.concatenate(
        (
            tok_rows.reshape(expert_list, capacity, width_dev),
            grad_rows.reshape(expert_list, capacity, width_dev),
        ),
        axis=1,
    )
    got = lax.all_to_all(send, ("y_lo", "z_hi"), split_axis=0, concat_axis=0, tiled=True)
    tok_own = got[:, :capacity].reshape(rows, width_dev)
    grad_own = got[:, capacity:].reshape(rows, width_dev)

    paired_own = jnp.concatenate((gate_up[0], gate_up[1]), axis=1)
    paired_own, down_late, tok_own, grad_own = lax.optimization_barrier(
        (paired_own, down, tok_own, grad_own)
    )
    tok_left = shift(tok_own, 1)
    grad_right = shift(grad_own, -1)
    tok_right = shift(tok_own, -1)
    grad_left = shift(grad_own, 1)
    paired_far = swap(paired_own, "z_lo")
    down_far = swap(down_late, "z_lo")
    tok_across = shift(tok_left, 1)
    grad_across = shift(grad_right, -1)
    paired = jnp.concatenate((paired_own, paired_far), axis=1)
    downs = jnp.concatenate((down, down_far), axis=0)

    tok_all = jnp.concatenate((tok_own, tok_left, tok_right, tok_across), axis=0)
    grad_all = jnp.concatenate((grad_own, grad_left, grad_right, grad_across), axis=0)

    pre = jnp.concatenate(
        (f32_dot(tok_all, paired, ((1,), (0,))), f32_dot(grad_all, downs, ((1,), (1,)))), axis=1
    )
    core = lax.axis_index("core")
    y_hi = lax.axis_index("y_hi")
    half = pre.shape[0] // 2
    keep = jnp.where(core == 0, pre[:half], pre[half:])
    other = to_bf16(jnp.where(core == 0, pre[half:], pre[:half]))
    keep = keep + swap(other, "core").astype(jnp.float32)
    quarter = half // 2
    other = to_bf16(jnp.where(y_hi == 0, keep[quarter:], keep[:quarter]))
    keep = jnp.where(y_hi == 0, keep[:quarter], keep[quarter:])
    keep = keep + swap(other, "y_hi").astype(jnp.float32)

    def block(first):
        return jnp.concatenate(
            (keep[:, first : first + hidden], keep[:, first + 2 * hidden : first + 3 * hidden]),
            axis=1,
        )

    gate_pre = block(0)
    up_pre = block(hidden)
    back = keep[:, 4 * hidden :]
    sigmoid_gate = jax.nn.sigmoid(gate_pre)
    silu_gate = gate_pre * sigmoid_gate
    scaled = to_bf16(silu_gate * up_pre)
    d_gate = to_bf16(back * up_pre * sigmoid_gate * (1.0 + gate_pre * (1.0 - sigmoid_gate)))
    d_up = to_bf16(back * silu_gate)
    points = jnp.concatenate(
        (d_gate[:, :hidden], d_up[:, :hidden], d_gate[:, hidden:], d_up[:, hidden:], scaled), axis=1
    )
    far = swap(points, "y_hi")
    points = jnp.where(
        y_hi == 0, jnp.concatenate((points, far), axis=0), jnp.concatenate((far, points), axis=0)
    )
    far = swap(points, "core")
    points = jnp.where(
        core == 0, jnp.concatenate((points, far), axis=0), jnp.concatenate((far, points), axis=0)
    )
    d_paired = points[:, : 4 * hidden]
    scaled = points[:, 4 * hidden :]

    mixed_part = f32_dot(scaled, downs, ((1,), (0,)))
    delta_part = f32_dot(d_paired, paired, ((1,), (1,)))

    def part(value, chunk):
        return value[chunk * rows : (chunk + 1) * rows]

    mixed_in = shift(to_bf16(part(mixed_part, 3)), 1)
    delta_in = shift(to_bf16(part(delta_part, 3)), -1)
    mixed_b = shift(to_bf16(part(mixed_part, 1)), -1)
    delta_b = shift(to_bf16(part(delta_part, 2)), 1)
    mixed_a = shift(to_bf16(part(mixed_part, 2) + mixed_in.astype(jnp.float32)), 1)
    delta_a = shift(to_bf16(part(delta_part, 1) + delta_in.astype(jnp.float32)), -1)
    mixed_sum = to_bf16(
        part(mixed_part, 0) + mixed_a.astype(jnp.float32) + mixed_b.astype(jnp.float32)
    )
    delta_sum = to_bf16(
        part(delta_part, 0) + delta_a.astype(jnp.float32) + delta_b.astype(jnp.float32)
    )

    grad_paired_far = to_bf16(f32_dot(tok_all, d_paired[:, 2 * hidden :], ((0,), (0,))))
    grad_down_far = to_bf16(f32_dot(scaled[:, hidden:], grad_all, ((0,), (0,))))
    grad_paired_in = swap(grad_paired_far, "z_lo")
    grad_down_in = swap(grad_down_far, "z_lo")
    grad_paired = f32_dot(tok_all, d_paired[:, : 2 * hidden], ((0,), (0,)))
    grad_paired = grad_paired + grad_paired_in.astype(jnp.float32)
    grad_down = f32_dot(scaled[:, :hidden], grad_all, ((0,), (0,)))
    grad_down = grad_down + grad_down_in.astype(jnp.float32)
    grad_stack = jnp.stack((grad_paired[:, :hidden], grad_paired[:, hidden:]), axis=0)
    gate_up_new, gate_up_m_new, gate_up_v_new = adamw(gate_up, gate_up_m, gate_up_v, grad_stack)
    down_new, down_m_new, down_v_new = adamw(down, down_m, down_v, grad_down)

    back_send = jnp.concatenate(
        (
            mixed_sum.reshape(expert_list, capacity, width_dev),
            delta_sum.reshape(expert_list, capacity, width_dev),
        ),
        axis=1,
    )
    returned = lax.all_to_all(back_send, ("y_lo", "z_hi"), split_axis=0, concat_axis=0, tiled=True)
    mixed_rows = returned[:, :capacity].reshape(rows, width_dev)
    delta_rows = returned[:, capacity:].reshape(rows, width_dev)
    mixed = to_bf16(f32_dot(gate_selector, mixed_rows, ((0,), (0,))))
    grad_tokens = to_bf16(f32_dot(selector, delta_rows, ((0,), (0,))))
    return (
        mixed,
        grad_tokens,
        gate_up_new,
        gate_up_m_new,
        gate_up_v_new,
        down_new,
        down_m_new,
        down_v_new,
    )


def solution(mesh):
    pipe = ("y_hi", "core")
    expert = ("y_lo", "z_hi", "z_lo", "x")
    fine = Mesh(mesh.devices.reshape(2, 2, 2, 4, 2, 4), pipe + expert)
    rows_spec = P(expert, pipe)
    route_spec = P(expert, None)
    cols_spec = P(None, pipe, expert)
    return jax.shard_map(
        per_device,
        mesh=fine,
        in_specs=(
            rows_spec,
            rows_spec,
            route_spec,
            route_spec,
            cols_spec,
            cols_spec,
            cols_spec,
            rows_spec,
            rows_spec,
            rows_spec,
        ),
        out_specs=(
            rows_spec,
            rows_spec,
            cols_spec,
            cols_spec,
            cols_spec,
            rows_spec,
            rows_spec,
            rows_spec,
        ),
        check_vma=False,
    )
```

```python
import jax
import jax.numpy as jnp
from jax import lax
from jax.sharding import Mesh
from jax.sharding import PartitionSpec as P


beta_first = 0.9
beta_second = 0.95
learning_rate = 0.00022
decay_rate = 0.1
epsilon = 1e-08


def adamw(weight, moment_one, moment_two, gradient):
    weight_real = weight.astype(jnp.float32)
    first_new = beta_first * moment_one.astype(jnp.float32) + (1.0 - beta_first) * gradient
    second_new = (
        beta_second * moment_two.astype(jnp.float32) + (1.0 - beta_second) * gradient * gradient
    )
    weight_new = weight_real - learning_rate * (
        first_new / (jnp.sqrt(second_new) + epsilon) + decay_rate * weight_real
    )
    return (
        weight_new.astype(jnp.bfloat16),
        first_new.astype(jnp.bfloat16),
        second_new.astype(jnp.bfloat16),
    )


def f32_dot(left, right, dims):
    return lax.dot_general(left, right, (dims, ((), ())), preferred_element_type=jnp.float32)


def swap(value, axis):
    return lax.ppermute(value, axis, [(0, 1), (1, 0)])


def shift(value, step):
    size = lax.axis_size("x")
    return lax.ppermute(value, "x", [(i, (i + step) % size) for i in range(size)])


def after(value, *earlier):
    return lax.optimization_barrier((value,) + earlier)[0]


def to_bf16(value):
    return value.astype(jnp.bfloat16)


def per_device(
    tokens,
    grad_out,
    routed_expert_index,
    route_gates,
    gate_up,
    gate_up_m,
    gate_up_v,
    down,
    down_m,
    down_v,
):
    expert_list = lax.axis_size("y_lo") * lax.axis_size("z_hi")
    tok_dev, width_dev = tokens.shape
    hidden = gate_up.shape[2]
    capacity = 16
    rows = expert_list * capacity

    experts = jnp.arange(expert_list, dtype=jnp.int32)[:, None, None]
    index_t = routed_expert_index.T
    gates_t = route_gates.T.astype(jnp.float32)
    named = (index_t[None] == experts).astype(jnp.float32)
    member = jnp.sum(named, axis=1)
    gate_of = jnp.sum(named * gates_t[None], axis=1)
    earlier = (
        lax.broadcasted_iota(jnp.int32, (tok_dev, tok_dev), 0)
        < lax.broadcasted_iota(jnp.int32, (tok_dev, tok_dev), 1)
    ).astype(jnp.bfloat16)
    slot = f32_dot(to_bf16(member), earlier, ((1,), (0,))).astype(jnp.int32)
    slots = lax.broadcasted_iota(jnp.int32, (expert_list, capacity, tok_dev), 1)
    here = (slots == slot[:, None, :]) & (member[:, None, :] > 0.5)
    selector = here.astype(jnp.bfloat16).reshape(rows, tok_dev)
    gate_selector = to_bf16(jnp.where(here, gate_of[:, None, :], 0.0)).reshape(rows, tok_dev)

    core = lax.axis_index("core")
    y_hi = lax.axis_index("y_hi")
    mid = rows // 2

    def exchange(first, second):
        pair = jnp.concatenate(
            (
                first.reshape(expert_list, capacity, width_dev),
                second.reshape(expert_list, capacity, width_dev),
            ),
            axis=1,
        )
        return lax.all_to_all(pair, ("y_lo", "z_hi"), split_axis=0, concat_axis=0, tiled=True)

    def core_sum(low, high):
        keep = jnp.where(core == 0, low, high)
        return keep + swap(jnp.where(core == 0, high, low), "core")

    def y_sum(keep):
        return keep + swap(to_bf16(keep), "y_hi").astype(jnp.float32)

    def core_gather(points):
        far = swap(points, "core")
        return jnp.where(
            core == 0,
            jnp.concatenate((points, far), axis=0),
            jnp.concatenate((far, points), axis=0),
        )

    def both(value, first):
        return jnp.concatenate(
            (value[:, first : first + hidden], value[:, first + 2 * hidden : first + 3 * hidden]),
            axis=1,
        )

    nothing = jnp.zeros_like(here, dtype=jnp.bfloat16)
    sel3 = here.astype(jnp.bfloat16)
    gate3 = gate_selector.reshape(sel3.shape)
    combine = jnp.concatenate(
        (
            jnp.concatenate((gate3, nothing), axis=2),
            jnp.concatenate((nothing, sel3), axis=2),
        ),
        axis=1,
    ).reshape(2 * rows, 2 * tok_dev)

    tok_rows = to_bf16(f32_dot(selector, tokens, ((1,), (0,))))
    grad_rows = to_bf16(f32_dot(gate_selector, grad_out, ((1,), (0,))))
    got = exchange(tok_rows, grad_rows)
    tok_own = got[:, :capacity].reshape(rows, width_dev)
    grad_own = got[:, capacity:].reshape(rows, width_dev)
    tok_own, grad_own, gate, up, down_late, combine = lax.optimization_barrier(
        (tok_own, grad_own, gate_up[0], gate_up[1], down, combine)
    )
    paired_own = jnp.concatenate((gate, up), axis=1)
    tok_left = shift(tok_own, 1)
    tok_right = shift(tok_own, -1)
    paired_far = swap(paired_own, "z_lo")
    tok_across = shift(tok_left, 1)
    grad_right = shift(after(grad_own, tok_right), -1)
    grad_left = shift(after(grad_own, tok_left), 1)
    grad_across = shift(grad_right, -1)
    down_far = swap(down_late, "z_lo")
    paired = jnp.concatenate((paired_own, paired_far), axis=1)
    downs = jnp.concatenate((down, down_far), axis=0)
    tok_low = jnp.concatenate((tok_own, tok_left), axis=0)
    tok_high = jnp.concatenate((tok_right, tok_across), axis=0)
    grad_low = jnp.concatenate((grad_own, grad_left), axis=0)
    grad_high = jnp.concatenate((grad_right, grad_across), axis=0)
    tok_all = jnp.concatenate((tok_low, tok_high), axis=0)
    grad_all = jnp.concatenate((grad_low, grad_high), axis=0)

    pre = y_sum(
        core_sum(
            f32_dot(tok_low, paired, ((1,), (0,))), f32_dot(tok_high, paired, ((1,), (0,)))
        )
    )
    gate_pre = both(pre, 0)
    up_pre = both(pre, hidden)
    sigmoid_gate = jax.nn.sigmoid(gate_pre)
    silu_gate = gate_pre * sigmoid_gate
    scaled = core_gather(to_bf16(silu_gate * up_pre))

    def scatter_x(value, step):
        chunks = [value[i * rows : (i + 1) * rows] for i in range(4)]
        near, back_near = (chunks[2], chunks[1]) if step == 1 else (chunks[1], chunks[2])
        across = shift(to_bf16(chunks[3]), step).astype(jnp.float32)
        other = shift(to_bf16(back_near), -step).astype(jnp.float32)
        one = shift(to_bf16(near + across), step).astype(jnp.float32)
        return to_bf16(chunks[0] + one + other)

    mixed_part = f32_dot(scaled, downs, ((1,), (0,)))
    mixed_sum = scatter_x(mixed_part, 1)

    grad_low = after(grad_low, scaled)
    back = y_sum(
        core_sum(f32_dot(grad_low, downs, ((1,), (1,))), f32_dot(grad_high, downs, ((1,), (1,))))
    )
    back, up_pre, gate_pre = lax.optimization_barrier((back, up_pre, gate_pre))
    sigmoid_gate = jax.nn.sigmoid(gate_pre)
    silu_gate = gate_pre * sigmoid_gate
    d_gate = to_bf16(back * up_pre * sigmoid_gate * (1.0 + gate_pre * (1.0 - sigmoid_gate)))
    d_up = to_bf16(back * silu_gate)
    d_paired = core_gather(
        jnp.concatenate(
            (d_gate[:, :hidden], d_up[:, :hidden], d_gate[:, hidden:], d_up[:, hidden:]), axis=1
        )
    )
    delta_sum = scatter_x(f32_dot(d_paired, paired, ((1,), (1,))), -1)
    returned = exchange(mixed_sum, delta_sum)

    grad_down_far = to_bf16(f32_dot(scaled[:, hidden:], grad_all, ((0,), (0,))))
    grad_down_in = swap(grad_down_far, "z_lo")
    grad_paired_far = to_bf16(f32_dot(tok_all, d_paired[:, 2 * hidden :], ((0,), (0,))))
    grad_paired_in = swap(grad_paired_far, "z_lo")
    grad_paired = f32_dot(tok_all, d_paired[:, : 2 * hidden], ((0,), (0,)))
    grad_paired = grad_paired + grad_paired_in.astype(jnp.float32)
    grad_down = f32_dot(scaled[:, :hidden], grad_all, ((0,), (0,)))
    grad_down = grad_down + grad_down_in.astype(jnp.float32)
    grad_stack = jnp.stack((grad_paired[:, :hidden], grad_paired[:, hidden:]), axis=0)
    gate_up_new, gate_up_m_new, gate_up_v_new = adamw(gate_up, gate_up_m, gate_up_v, grad_stack)
    down_new, down_m_new, down_v_new = adamw(down, down_m, down_v, grad_down)

    combined = to_bf16(
        f32_dot(combine, returned.reshape(2 * rows, width_dev), ((0,), (0,)))
    )
    mixed = combined[:tok_dev]
    grad_tokens = combined[tok_dev:]
    return (
        mixed,
        grad_tokens,
        gate_up_new,
        gate_up_m_new,
        gate_up_v_new,
        down_new,
        down_m_new,
        down_v_new,
    )


def solution(mesh):
    pipe = ("y_hi", "core")
    expert = ("y_lo", "z_hi", "z_lo", "x")
    fine = Mesh(mesh.devices.reshape(2, 2, 2, 4, 2, 4), pipe + expert)
    rows_spec = P(expert, pipe)
    route_spec = P(expert, None)
    cols_spec = P(None, pipe, expert)
    return jax.shard_map(
        per_device,
        mesh=fine,
        in_specs=(
            rows_spec,
            rows_spec,
            route_spec,
            route_spec,
            cols_spec,
            cols_spec,
            cols_spec,
            rows_spec,
            rows_spec,
            rows_spec,
        ),
        out_specs=(
            rows_spec,
            rows_spec,
            cols_spec,
            cols_spec,
            cols_spec,
            rows_spec,
            rows_spec,
            rows_spec,
        ),
        check_vma=False,
    )
```

```python
import jax
import jax.numpy as jnp
from jax import lax
from jax.experimental import pallas as pl
from jax.sharding import Mesh
from jax.sharding import PartitionSpec as P


beta_first = 0.9
beta_second = 0.95
learning_rate = 0.00022
decay_rate = 0.1
epsilon = 1e-08


def adamw(weight, moment_one, moment_two, gradient):
    weight_real = weight.astype(jnp.float32)
    first_new = beta_first * moment_one.astype(jnp.float32) + (1.0 - beta_first) * gradient
    second_new = (
        beta_second * moment_two.astype(jnp.float32) + (1.0 - beta_second) * gradient * gradient
    )
    weight_new = weight_real - learning_rate * (
        first_new / (jnp.sqrt(second_new) + epsilon) + decay_rate * weight_real
    )
    return (
        weight_new.astype(jnp.bfloat16),
        first_new.astype(jnp.bfloat16),
        second_new.astype(jnp.bfloat16),
    )


def f32_dot(left, right, dims):
    return lax.dot_general(left, right, (dims, ((), ())), preferred_element_type=jnp.float32)


def swap(value, axis):
    return lax.ppermute(value, axis, [(0, 1), (1, 0)])


def shift(value, step):
    size = lax.axis_size("x")
    return lax.ppermute(value, "x", [(i, (i + step) % size) for i in range(size)])


def after(value, *earlier):
    return lax.optimization_barrier((value,) + earlier)[0]


def to_bf16(value):
    return value.astype(jnp.bfloat16)


EXPERTS = 8
CAPACITY = 16


def dispatch_kernel(index_ref, gates_ref, tokens_ref, grads_ref, send_ref, combine_ref):
    index = index_ref[...]
    gates = gates_ref[...].astype(jnp.float32)
    count = index.shape[1]
    hits = [index == e for e in range(EXPERTS)]
    members = [jnp.sum(jnp.where(hit, 1.0, 0.0), axis=0, keepdims=True) for hit in hits]
    gate_rows = [jnp.sum(jnp.where(hit, gates, 0.0), axis=0, keepdims=True) for hit in hits]
    member = jnp.concatenate(members, axis=0)
    earlier = lax.broadcasted_iota(jnp.int32, (count, count), 0) < lax.broadcasted_iota(
        jnp.int32, (count, count), 1
    )
    slot = f32_dot(
        member.astype(jnp.bfloat16),
        jnp.where(earlier, 1.0, 0.0).astype(jnp.bfloat16),
        ((1,), (0,)),
    )
    slots = lax.broadcasted_iota(jnp.int32, (CAPACITY, count), 0).astype(jnp.float32)
    select, weigh = [], []
    for e in range(EXPERTS):
        here = (slots == slot[e : e + 1]) & (member[e : e + 1] > 0.5)
        select.append(jnp.where(here, 1.0, 0.0))
        weigh.append(jnp.where(here, gate_rows[e], 0.0))
    select = jnp.concatenate(select, axis=0).astype(jnp.bfloat16)
    weigh = jnp.concatenate(weigh, axis=0).astype(jnp.bfloat16)
    token_rows = f32_dot(select, tokens_ref[...], ((1,), (0,))).astype(jnp.bfloat16)
    grad_rows = f32_dot(weigh, grads_ref[...], ((1,), (0,))).astype(jnp.bfloat16)
    combine_ref[...] = jnp.zeros(combine_ref.shape, jnp.bfloat16)
    for e in range(EXPERTS):
        rows = slice(e * CAPACITY, (e + 1) * CAPACITY)
        send_ref[e, :CAPACITY, :] = token_rows[rows]
        send_ref[e, CAPACITY:, :] = grad_rows[rows]
        combine_ref[e, :CAPACITY, :count] = weigh[rows]
        combine_ref[e, CAPACITY:, count:] = select[rows]


def per_device(
    tokens,
    grad_out,
    routed_expert_index,
    route_gates,
    gate_up,
    gate_up_m,
    gate_up_v,
    down,
    down_m,
    down_v,
):
    expert_list = EXPERTS
    tok_dev, width_dev = tokens.shape
    hidden = gate_up.shape[2]
    capacity = CAPACITY
    rows = expert_list * capacity

    send, combine = pl.pallas_call(
        dispatch_kernel,
        out_shape=(
            jax.ShapeDtypeStruct((expert_list, 2 * capacity, width_dev), jnp.bfloat16),
            jax.ShapeDtypeStruct((expert_list, 2 * capacity, 2 * tok_dev), jnp.bfloat16),
        ),
        name="dispatch",
    )(routed_expert_index.T, route_gates.T, tokens, grad_out)
    combine = combine.reshape(2 * rows, 2 * tok_dev)

    core = lax.axis_index("core")
    y_hi = lax.axis_index("y_hi")
    mid = rows // 2

    def exchange(pair):
        return lax.all_to_all(pair, ("y_lo", "z_hi"), split_axis=0, concat_axis=0, tiled=True)

    def interleave(first, second):
        shape = (expert_list, capacity, width_dev)
        return jnp.concatenate((first.reshape(shape), second.reshape(shape)), axis=1)

    def core_sum(low, high):
        keep = jnp.where(core == 0, low, high)
        return keep + swap(jnp.where(core == 0, high, low), "core")

    def y_sum(keep):
        return keep + swap(to_bf16(keep), "y_hi").astype(jnp.float32)

    def core_gather(points):
        far = swap(points, "core")
        return jnp.where(
            core == 0,
            jnp.concatenate((points, far), axis=0),
            jnp.concatenate((far, points), axis=0),
        )

    def both(value, first):
        return jnp.concatenate(
            (value[:, first : first + hidden], value[:, first + 2 * hidden : first + 3 * hidden]),
            axis=1,
        )

    got = exchange(send)
    tok_own = got[:, :capacity].reshape(rows, width_dev)
    grad_own = got[:, capacity:].reshape(rows, width_dev)
    tok_own, grad_own, gate, up, down_late, combine = lax.optimization_barrier(
        (tok_own, grad_own, gate_up[0], gate_up[1], down, combine)
    )
    paired_own = jnp.concatenate((gate, up), axis=1)
    tok_left = shift(tok_own, 1)
    tok_right = shift(tok_own, -1)
    paired_far = swap(paired_own, "z_lo")
    tok_across = shift(tok_left, 1)
    grad_right = shift(after(grad_own, tok_right), -1)
    grad_left = shift(after(grad_own, tok_left), 1)
    grad_across = shift(grad_right, -1)
    down_far = swap(down_late, "z_lo")
    paired = jnp.concatenate((paired_own, paired_far), axis=1)
    downs = jnp.concatenate((down, down_far), axis=0)
    tok_low = jnp.concatenate((tok_own, tok_left), axis=0)
    tok_high = jnp.concatenate((tok_right, tok_across), axis=0)
    grad_low = jnp.concatenate((grad_own, grad_left), axis=0)
    grad_high = jnp.concatenate((grad_right, grad_across), axis=0)
    tok_all = jnp.concatenate((tok_low, tok_high), axis=0)
    grad_all = jnp.concatenate((grad_low, grad_high), axis=0)

    pre = y_sum(
        core_sum(
            f32_dot(tok_low, paired, ((1,), (0,))), f32_dot(tok_high, paired, ((1,), (0,)))
        )
    )
    gate_pre = both(pre, 0)
    up_pre = both(pre, hidden)
    sigmoid_gate = jax.nn.sigmoid(gate_pre)
    silu_gate = gate_pre * sigmoid_gate
    scaled = core_gather(to_bf16(silu_gate * up_pre))

    def scatter_x(value, step):
        chunks = [value[i * rows : (i + 1) * rows] for i in range(4)]
        near, back_near = (chunks[2], chunks[1]) if step == 1 else (chunks[1], chunks[2])
        across = shift(to_bf16(chunks[3]), step).astype(jnp.float32)
        other = shift(to_bf16(back_near), -step).astype(jnp.float32)
        one = shift(to_bf16(near + across), step).astype(jnp.float32)
        return to_bf16(chunks[0] + one + other)

    mixed_part = f32_dot(scaled, downs, ((1,), (0,)))
    mixed_sum = scatter_x(mixed_part, 1)

    grad_low = after(grad_low, scaled)
    back = y_sum(
        core_sum(f32_dot(grad_low, downs, ((1,), (1,))), f32_dot(grad_high, downs, ((1,), (1,))))
    )
    back, up_pre, gate_pre = lax.optimization_barrier((back, up_pre, gate_pre))
    sigmoid_gate = jax.nn.sigmoid(gate_pre)
    silu_gate = gate_pre * sigmoid_gate
    d_gate = to_bf16(back * up_pre * sigmoid_gate * (1.0 + gate_pre * (1.0 - sigmoid_gate)))
    d_up = to_bf16(back * silu_gate)
    d_paired = core_gather(
        jnp.concatenate(
            (d_gate[:, :hidden], d_up[:, :hidden], d_gate[:, hidden:], d_up[:, hidden:]), axis=1
        )
    )
    delta_sum = scatter_x(f32_dot(d_paired, paired, ((1,), (1,))), -1)
    returned = exchange(interleave(mixed_sum, delta_sum))

    grad_down_far = to_bf16(f32_dot(scaled[:, hidden:], grad_all, ((0,), (0,))))
    grad_down_in = swap(grad_down_far, "z_lo")
    grad_paired_far = to_bf16(f32_dot(tok_all, d_paired[:, 2 * hidden :], ((0,), (0,))))
    grad_paired_in = swap(grad_paired_far, "z_lo")
    grad_paired = f32_dot(tok_all, d_paired[:, : 2 * hidden], ((0,), (0,)))
    grad_paired = grad_paired + grad_paired_in.astype(jnp.float32)
    grad_down = f32_dot(scaled[:, :hidden], grad_all, ((0,), (0,)))
    grad_down = grad_down + grad_down_in.astype(jnp.float32)
    grad_stack = jnp.stack((grad_paired[:, :hidden], grad_paired[:, hidden:]), axis=0)
    gate_up_new, gate_up_m_new, gate_up_v_new = adamw(gate_up, gate_up_m, gate_up_v, grad_stack)
    down_new, down_m_new, down_v_new = adamw(down, down_m, down_v, grad_down)

    combined = to_bf16(
        f32_dot(combine, returned.reshape(2 * rows, width_dev), ((0,), (0,)))
    )
    mixed = combined[:tok_dev]
    grad_tokens = combined[tok_dev:]
    return (
        mixed,
        grad_tokens,
        gate_up_new,
        gate_up_m_new,
        gate_up_v_new,
        down_new,
        down_m_new,
        down_v_new,
    )


def solution(mesh):
    pipe = ("y_hi", "core")
    expert = ("y_lo", "z_hi", "z_lo", "x")
    fine = Mesh(mesh.devices.reshape(2, 2, 2, 4, 2, 4), pipe + expert)
    rows_spec = P(expert, pipe)
    route_spec = P(expert, None)
    cols_spec = P(None, pipe, expert)
    return jax.shard_map(
        per_device,
        mesh=fine,
        in_specs=(
            rows_spec,
            rows_spec,
            route_spec,
            route_spec,
            cols_spec,
            cols_spec,
            cols_spec,
            rows_spec,
            rows_spec,
            rows_spec,
        ),
        out_specs=(
            rows_spec,
            rows_spec,
            cols_spec,
            cols_spec,
            cols_spec,
            rows_spec,
            rows_spec,
            rows_spec,
        ),
        check_vma=False,
    )
```

```python
import jax
import jax.numpy as jnp
from jax import lax
from jax.experimental import pallas as pl
from jax.sharding import Mesh
from jax.sharding import PartitionSpec as P


beta_first = 0.9
beta_second = 0.95
learning_rate = 0.00022
decay_rate = 0.1
epsilon = 1e-08


def adamw(weight, moment_one, moment_two, gradient):
    weight_real = weight.astype(jnp.float32)
    first_new = beta_first * moment_one.astype(jnp.float32) + (1.0 - beta_first) * gradient
    second_new = (
        beta_second * moment_two.astype(jnp.float32) + (1.0 - beta_second) * gradient * gradient
    )
    weight_new = weight_real - learning_rate * (
        first_new / (jnp.sqrt(second_new) + epsilon) + decay_rate * weight_real
    )
    return (
        weight_new.astype(jnp.bfloat16),
        first_new.astype(jnp.bfloat16),
        second_new.astype(jnp.bfloat16),
    )


def f32_dot(left, right, dims):
    return lax.dot_general(left, right, (dims, ((), ())), preferred_element_type=jnp.float32)


def swap(value, axis):
    return lax.ppermute(value, axis, [(0, 1), (1, 0)])


def shift(value, step):
    size = lax.axis_size("x")
    return lax.ppermute(value, "x", [(i, (i + step) % size) for i in range(size)])


def after(value, *earlier):
    return lax.optimization_barrier((value,) + earlier)[0]


def to_bf16(value):
    return value.astype(jnp.bfloat16)


EXPERTS = 8
CAPACITY = 16


def dispatch_kernel(index_ref, gates_ref, tokens_ref, grads_ref, send_ref, combine_ref):
    index = index_ref[...]
    gates = gates_ref[...].astype(jnp.float32)
    count = index.shape[1]
    hits = [index == e for e in range(EXPERTS)]
    members = [jnp.sum(jnp.where(hit, 1.0, 0.0), axis=0, keepdims=True) for hit in hits]
    gate_rows = [jnp.sum(jnp.where(hit, gates, 0.0), axis=0, keepdims=True) for hit in hits]
    member = jnp.concatenate(members, axis=0)
    earlier = lax.broadcasted_iota(jnp.int32, (count, count), 0) < lax.broadcasted_iota(
        jnp.int32, (count, count), 1
    )
    slot = f32_dot(
        member.astype(jnp.bfloat16),
        jnp.where(earlier, 1.0, 0.0).astype(jnp.bfloat16),
        ((1,), (0,)),
    )
    slots = lax.broadcasted_iota(jnp.int32, (CAPACITY, count), 0).astype(jnp.float32)
    select, weigh = [], []
    for e in range(EXPERTS):
        here = (slots == slot[e : e + 1]) & (member[e : e + 1] > 0.5)
        select.append(jnp.where(here, 1.0, 0.0))
        weigh.append(jnp.where(here, gate_rows[e], 0.0))
    select = jnp.concatenate(select, axis=0).astype(jnp.bfloat16)
    weigh = jnp.concatenate(weigh, axis=0).astype(jnp.bfloat16)
    token_rows = f32_dot(select, tokens_ref[...], ((1,), (0,))).astype(jnp.bfloat16)
    grad_rows = f32_dot(weigh, grads_ref[...], ((1,), (0,))).astype(jnp.bfloat16)
    combine_ref[...] = jnp.zeros(combine_ref.shape, jnp.bfloat16)
    for e in range(EXPERTS):
        rows = slice(e * CAPACITY, (e + 1) * CAPACITY)
        send_ref[e, :CAPACITY, :] = token_rows[rows]
        send_ref[e, CAPACITY:, :] = grad_rows[rows]
        combine_ref[e, :CAPACITY, :count] = weigh[rows]
        combine_ref[e, CAPACITY:, count:] = select[rows]


def per_device(
    tokens,
    grad_out,
    routed_expert_index,
    route_gates,
    gate_up,
    gate_up_m,
    gate_up_v,
    down,
    down_m,
    down_v,
):
    expert_list = EXPERTS
    tok_dev, width_dev = tokens.shape
    hidden = gate_up.shape[2]
    capacity = CAPACITY
    rows = expert_list * capacity

    send, combine = pl.pallas_call(
        dispatch_kernel,
        out_shape=(
            jax.ShapeDtypeStruct((expert_list, 2 * capacity, width_dev), jnp.bfloat16),
            jax.ShapeDtypeStruct((expert_list, 2 * capacity, 2 * tok_dev), jnp.bfloat16),
        ),
        name="dispatch",
    )(routed_expert_index.T, route_gates.T, tokens, grad_out)
    combine = combine.reshape(2 * rows, 2 * tok_dev)

    core = lax.axis_index("core")
    y_hi = lax.axis_index("y_hi")
    mid = rows // 2

    def exchange(pair):
        return lax.all_to_all(pair, ("y_lo", "z_hi"), split_axis=0, concat_axis=0, tiled=True)

    def interleave(first, second):
        shape = (expert_list, capacity, width_dev)
        return jnp.concatenate((first.reshape(shape), second.reshape(shape)), axis=1)

    def core_sum(low, high):
        keep = jnp.where(core == 0, low, high)
        return keep + swap(jnp.where(core == 0, high, low), "core")

    def y_sum(keep):
        return keep + swap(to_bf16(keep), "y_hi").astype(jnp.float32)

    def core_gather(points):
        far = swap(points, "core")
        return jnp.where(
            core == 0,
            jnp.concatenate((points, far), axis=0),
            jnp.concatenate((far, points), axis=0),
        )

    def both(value, first):
        return jnp.concatenate(
            (value[:, first : first + hidden], value[:, first + 2 * hidden : first + 3 * hidden]),
            axis=1,
        )

    got = exchange(send)
    tok_own = got[:, :capacity].reshape(rows, width_dev)
    grad_own = got[:, capacity:].reshape(rows, width_dev)
    tok_own, grad_own, gate, up, down_late, combine = lax.optimization_barrier(
        (tok_own, grad_own, gate_up[0], gate_up[1], down, combine)
    )
    paired_own = jnp.concatenate((gate, up), axis=1)
    tok_left = shift(tok_own, 1)
    tok_right = shift(tok_own, -1)
    paired_far = swap(paired_own, "z_lo")
    tok_across = shift(tok_left, 1)
    grad_right = shift(after(grad_own, tok_right), -1)
    grad_left = shift(after(grad_own, tok_left), 1)
    grad_across = shift(grad_right, -1)
    down_far = swap(down_late, "z_lo")
    paired = jnp.concatenate((paired_own, paired_far), axis=1)
    downs = jnp.concatenate((down, down_far), axis=0)
    tok_low = jnp.concatenate((tok_own, tok_left), axis=0)
    tok_high = jnp.concatenate((tok_right, tok_across), axis=0)
    grad_low = jnp.concatenate((grad_own, grad_left), axis=0)
    grad_high = jnp.concatenate((grad_right, grad_across), axis=0)
    tok_all = jnp.concatenate((tok_low, tok_high), axis=0)
    grad_all = jnp.concatenate((grad_low, grad_high), axis=0)

    pre = y_sum(
        core_sum(
            f32_dot(tok_low, paired, ((1,), (0,))), f32_dot(tok_high, paired, ((1,), (0,)))
        )
    )
    gate_pre = both(pre, 0)
    up_pre = both(pre, hidden)
    sigmoid_gate = jax.nn.sigmoid(gate_pre)
    silu_gate = gate_pre * sigmoid_gate
    scaled = core_gather(to_bf16(silu_gate * up_pre))

    def scatter_x(value, step, earlier=None):
        chunks = [value[i * rows : (i + 1) * rows] for i in range(4)]
        near, back_near = (chunks[2], chunks[1]) if step == 1 else (chunks[1], chunks[2])
        across = shift(to_bf16(chunks[3]), step).astype(jnp.float32)
        other = shift(to_bf16(back_near), -step).astype(jnp.float32)
        if earlier is not None:
            across = after(across, earlier)
        one = shift(to_bf16(near + across), step).astype(jnp.float32)
        return to_bf16(chunks[0] + one + other), other

    mixed_part = f32_dot(scaled, downs, ((1,), (0,)))
    mixed_sum, mixed_near = scatter_x(mixed_part, 1)

    grad_low = after(grad_low, scaled)
    back = y_sum(
        core_sum(f32_dot(grad_low, downs, ((1,), (1,))), f32_dot(grad_high, downs, ((1,), (1,))))
    )
    back, up_pre, gate_pre = lax.optimization_barrier((back, up_pre, gate_pre))
    sigmoid_gate = jax.nn.sigmoid(gate_pre)
    silu_gate = gate_pre * sigmoid_gate
    d_gate = to_bf16(back * up_pre * sigmoid_gate * (1.0 + gate_pre * (1.0 - sigmoid_gate)))
    d_up = to_bf16(back * silu_gate)
    d_paired = core_gather(
        jnp.concatenate(
            (d_gate[:, :hidden], d_up[:, :hidden], d_gate[:, hidden:], d_up[:, hidden:]), axis=1
        )
    )
    delta_part = f32_dot(d_paired, paired, ((1,), (1,)))
    delta_sum = scatter_x(delta_part, -1, mixed_near)[0]
    returned = exchange(interleave(mixed_sum, delta_sum))

    grad_down_far = to_bf16(f32_dot(scaled[:, hidden:], grad_all, ((0,), (0,))))
    grad_down_in = swap(grad_down_far, "z_lo")
    grad_paired_far = to_bf16(f32_dot(tok_all, d_paired[:, 2 * hidden :], ((0,), (0,))))
    grad_paired_in = swap(grad_paired_far, "z_lo")
    grad_paired = f32_dot(tok_all, d_paired[:, : 2 * hidden], ((0,), (0,)))
    grad_paired = grad_paired + grad_paired_in.astype(jnp.float32)
    grad_down = f32_dot(scaled[:, :hidden], grad_all, ((0,), (0,)))
    grad_down = grad_down + grad_down_in.astype(jnp.float32)
    grad_stack = jnp.stack((grad_paired[:, :hidden], grad_paired[:, hidden:]), axis=0)
    gate_up_new, gate_up_m_new, gate_up_v_new = adamw(gate_up, gate_up_m, gate_up_v, grad_stack)
    down_new, down_m_new, down_v_new = adamw(down, down_m, down_v, grad_down)

    combined = to_bf16(
        f32_dot(combine, returned.reshape(2 * rows, width_dev), ((0,), (0,)))
    )
    mixed = combined[:tok_dev]
    grad_tokens = combined[tok_dev:]
    return (
        mixed,
        grad_tokens,
        gate_up_new,
        gate_up_m_new,
        gate_up_v_new,
        down_new,
        down_m_new,
        down_v_new,
    )


def solution(mesh):
    pipe = ("y_hi", "core")
    expert = ("y_lo", "z_hi", "z_lo", "x")
    fine = Mesh(mesh.devices.reshape(2, 2, 2, 4, 2, 4), pipe + expert)
    rows_spec = P(expert, pipe)
    route_spec = P(expert, None)
    cols_spec = P(None, pipe, expert)
    return jax.shard_map(
        per_device,
        mesh=fine,
        in_specs=(
            rows_spec,
            rows_spec,
            route_spec,
            route_spec,
            cols_spec,
            cols_spec,
            cols_spec,
            rows_spec,
            rows_spec,
            rows_spec,
        ),
        out_specs=(
            rows_spec,
            rows_spec,
            cols_spec,
            cols_spec,
            cols_spec,
            rows_spec,
            rows_spec,
            rows_spec,
        ),
        check_vma=False,
    )
```
